1024 devices in a mesh: gx: 4 (over x_hi, core), gy: 4 (over x_lo), gz: 64 (over z, y).
Axes of the slice: x: 8 (x_hi: 2, x_lo: 4; x = x_hi * 4 + x_lo), y: 8, z: 8, core: 2. Of those that a mesh axis runs over, the one named last changes fastest.
Arguments:
- positions: float32 [3, 4, 4, 128, 256], P(None, 'gx', 'gy', 'gz'), may hold values from 0 to 1
- velocities: float32 [3, 4, 4, 128, 256], P(None, 'gx', 'gy', 'gz'), may hold values from -2 to 2
- mass: float32 [4, 4, 128, 256], P('gx', 'gy', 'gz'), may hold values from 0.03 to 0.3
- counts: int32 [4, 4, 128], P('gx', 'gy', 'gz'), may hold values from 1 to 256, as said below
Outputs:
- new_positions: float32 [3, 4, 4, 128, 256], P(None, 'gx', 'gy', 'gz')
- new_velocities: float32 [3, 4, 4, 128, 256], P(None, 'gx', 'gy', 'gz')
The draws below stay inside these ranges and needn't reach their ends.
Inputs may be any that keep to these rules, and one draw needn't show every extreme that they name: `counts`: particles of a bin fill its first slots; every bin holds at least 128 particles, and some bin holds exactly 256 particles in every draw.
All inputs are finite; a program needn't handle non-finite values.
Results may differ from the reference program's by a relative error of at most 0.0001.
Values sent between devices are 32-bit elements; how exact they have to be, the bound alone decides.
A program may use at most 32 MiB of HBM per device.

```python
import math
import jax
import jax.numpy as jnp
from jax import lax

CAP = 256
SUBCYCLES = 2
NBX = 4
NBY = 4
NBZ = 128


def draw_counts(key, part):
    first_key, second_key, third_key = jax.random.split(key, 3)
    shape = (NBX, NBY, NBZ)
    first = jax.random.randint(first_key, shape, 0, CAP)
    second = jax.random.randint(second_key, shape, 0, CAP)
    filled = CAP // 2 + first * second // (2 * CAP)
    chosen = jax.random.randint(third_key, (), 0, NBX * NBY * NBZ)
    flat_index = lax.broadcasted_iota(jnp.int32, (NBX * NBY * NBZ,), 0).reshape(shape)
    return jnp.where(flat_index == chosen, CAP, filled).astype(jnp.int32)


def shard_levels(rng, extent, pieces, smallest, top_value):
    def one(position, parts):
        steps = jax.random.uniform(jax.random.fold_in(jax.random.fold_in(rng, 6), position), (parts,), jnp.float32, smallest / len(pieces), top_value / len(pieces))
        return jnp.repeat(jnp.exp(steps), extent[position] // parts).reshape((-1,) + (1,) * (len(extent) - position - 1))

    factor_of = one(*pieces[0])
    for cut in pieces[1:]:
        factor_of = factor_of * one(*cut)
    return factor_of


def centred(rng, dims, scale, most, shards=(), kind=jnp.bfloat16):
    level = shard_levels(rng, dims, shards, -0.22, 0.18) if shards else 1.0
    entries = jax.random.normal(rng, dims, jnp.float32) * scale * level
    return jnp.minimum(jnp.maximum(entries, -most), most).astype(kind)


def setup_inputs(seed: int = 0) -> dict:
    seeds = jax.random.split(jax.random.key(seed), 5)
    positions = jnp.clip(1.0 * jax.random.uniform(seeds[0], (3, NBX, NBY, NBZ, CAP), jnp.float32) ** shard_levels(seeds[0], (3, NBX, NBY, NBZ, CAP), ((1, 4), (2, 4), (3, 64)), -0.2, 0.2), 0.0, 1.0)
    velocities = centred(seeds[1], (3, NBX, NBY, NBZ, CAP), 0.3, 2.0, ((1, 4), (2, 4), (3, 64)), jnp.float32)
    mass = jnp.clip(jnp.exp(math.log(0.3) - 2.3025852 * jax.random.uniform(seeds[2], (NBX, NBY, NBZ, CAP), jnp.float32) ** shard_levels(seeds[2], (NBX, NBY, NBZ, CAP), ((0, 4), (1, 4), (2, 64)), -0.2, 0.2)), 0.03, 0.3)
    counts = draw_counts(jax.random.fold_in(seeds[4], 71), 0)
    return dict(positions=positions, velocities=velocities, mass=mass, counts=counts)


time_step = 0.25


def pair_forces(target, source, source_mass, offset):
    target_rows = jnp.moveaxis(target.reshape(3, -1, NBZ, CAP), 1, 0)
    source_rows = jnp.moveaxis(source.reshape(3, -1, NBZ, CAP), 1, 0)
    mass_rows = source_mass.reshape(-1, NBZ, CAP)

    def one_row(items):
        target_row, source_row, mass_row = items
        delta = offset[:, None, None, None] + source_row[:, :, None, :] - target_row[:, :, :, None]
        squared = jnp.sum(delta * delta, axis=0)
        falloff = jnp.maximum(1.0 - squared, 0.0)
        weighted = falloff * falloff * falloff * mass_row[:, None, :]
        return jnp.sum(delta * weighted[None], axis=-1)

    result = lax.map(one_row, (target_rows, source_rows, mass_rows))
    return jnp.moveaxis(result, 0, 1).reshape(target.shape)


def reference(positions, velocities, mass, counts):
    occupied = lax.broadcasted_iota(jnp.int32, mass.shape, 3) < counts[..., None]
    weight = jnp.where(occupied, mass, jnp.zeros_like(mass))
    place = positions
    speed = velocities
    for subcycle in range(SUBCYCLES):
        accel = jnp.zeros_like(place)
        for shift_x in (-1, 0, 1):
            for shift_y in (-1, 0, 1):
                for shift_z in (-1, 0, 1):
                    source = jnp.roll(place, (-shift_x, -shift_y, -shift_z), (1, 2, 3))
                    source_mass = jnp.roll(weight, (-shift_x, -shift_y, -shift_z), (0, 1, 2))
                    offset = jnp.array([shift_x, shift_y, shift_z], jnp.float32)
                    accel = accel + pair_forces(place, source, source_mass, offset)
        speed = speed + time_step * accel
        place = jnp.clip(place + time_step * speed, 0.0, 1.0)
    new_positions = jnp.where(occupied[None], place, jnp.zeros_like(place))
    new_velocities = jnp.where(occupied[None], speed, jnp.zeros_like(speed))
    return new_positions, new_velocities
```

```python
import functools

import jax
import jax.numpy as jnp
from jax import lax
from jax.experimental import pallas as pl
from jax.experimental.pallas import tpu as pltpu
from jax.sharding import PartitionSpec as P

SUBCYCLES = 2
LANES = 128
time_step = 0.25
MESH = pl.DeviceIdType.MESH


def row_index():
    return lax.broadcasted_iota(jnp.int32, (8, LANES), 0)


def split(value):
    scaled = value * 65537.0
    high = scaled - (scaled - value)
    return high, value - high


def over_components(value):
    value = value + pltpu.roll(value, 2, 0)
    return value + pltpu.roll(value, 4, 0)


def frame_offset(row, offset_x, offset_y, offset_z):
    return jnp.where(row < 2, offset_x, jnp.where(row < 4, offset_y, jnp.where(row < 6, offset_z, 0.0)))


def source_features(packed, offset):
    row = row_index()
    is_mass = row >= 6
    moved = packed + offset
    high, low = split(moved)
    spatial = jnp.where(is_mass, 0.0, moved)
    norm = -over_components(spatial * spatial)
    norm_high, rest = split(norm)
    norm_mid, norm_low = split(rest)
    high = jnp.where(is_mass, 1.0, high)
    low = jnp.where(is_mass, 1.0, low)
    norm_mid, norm_low = pltpu.roll(norm_mid, 2, 0), pltpu.roll(norm_low, 4, 0)
    norms = jnp.where(row < 2, norm_high, jnp.where(row < 4, norm_mid, jnp.where(row < 6, norm_low, 0.0)))
    features = jnp.concatenate([high, low, high, norms], axis=0)
    mass = over_components(jnp.where(is_mass, packed, 0.0))
    moment_high, moment_low = split(mass * jnp.where(is_mass, 1.0, moved))
    even = row % 2 == 0
    moments = jnp.concatenate(
        [
            jnp.concatenate([jnp.where(even, part, 0.0), jnp.where(even, 0.0, part)], axis=1)
            for part in (moment_high, moment_low)
        ],
        axis=0,
    )
    return features.T.astype(jnp.bfloat16), moments.astype(jnp.bfloat16)


def target_features(packed, offset):
    row = row_index()
    is_mass = row >= 6
    even = row % 2 == 0
    moved = jnp.where(is_mass, 0.0, packed + offset)
    sides = [[], []]
    for half in range(2):
        mine = jnp.where(even, moved, pltpu.roll(moved, 1, 0)) if half == 0 else jnp.where(even, pltpu.roll(moved, 7, 0), moved)
        first, rest = split(1.0 - over_components(mine * mine))
        second, third = split(rest)
        high, low = split(2.0 * mine)
        stacked = jnp.concatenate(
            [
                jnp.where(is_mass, first, high),
                jnp.where(is_mass, second, high),
                jnp.where(is_mass, third, low),
                jnp.where(is_mass, 0.0, 1.0),
            ],
            axis=0,
        )
        parity = lax.broadcasted_iota(jnp.int32, (32, LANES), 0) % 2
        for source_half in range(2):
            sides[source_half].append(jnp.where(parity == source_half, stacked, 0.0))
    return jnp.concatenate(sides[0] + sides[1], axis=1).astype(jnp.bfloat16)


def pair_sums(features, moments, targets):
    falloff = jnp.maximum(jnp.dot(features, targets, preferred_element_type=jnp.float32), 0.0)
    weighted = falloff * falloff * falloff
    weighted = jnp.concatenate([weighted[:, : 2 * LANES], weighted[:, 2 * LANES :]], axis=0)
    high = weighted.astype(jnp.bfloat16)
    low = (weighted - high.astype(jnp.float32)).astype(jnp.bfloat16)
    return jnp.dot(moments, high, preferred_element_type=jnp.float32) + jnp.dot(
        moments, low, preferred_element_type=jnp.float32
    )


def packed_accel(total, packed, offset):
    row = row_index()
    even = row % 2 == 0
    folded = total[:8] + total[8:]
    halves = []
    for half in range(2):
        part = folded[:, half * LANES : (half + 1) * LANES]
        halves.append(jnp.where(even, part + pltpu.roll(part, 7, 0), part + pltpu.roll(part, 1, 0)))
    sums = jnp.where(even, halves[0], halves[1])
    mass_sum = over_components(jnp.where(row >= 6, sums, 0.0))
    return jnp.where(row >= 6, 0.0, sums - (packed + offset) * mass_sum)


def step_kernel(
    sizes, positions, velocities, mass, counts, new_positions, new_velocities, bins, targets, total, send_sem, recv_sem
):
    me = [lax.axis_index(name) for name in ("gx", "gy", "gz")]
    near = 1 - 2 * (me[0] % 2)

    def shift(xi, yi):
        return near * (xi % 2) - near * (xi // 2), (yi % 2) - (yi // 2)

    def neighbour(xi, yi, dz):
        dx, dy = shift(xi, yi)
        return tuple(lax.rem(at + d + size, size) for at, d, size in zip(me, (dx, dy, dz), sizes))

    peers = [
        (xi, yi, zi)
        for xi in (2, 1, 0)
        for yi in (1, 2, 0)
        for zi in (1, 2, 0)
        if (xi, yi, zi) != (0, 0, 0)
    ]
    shift_z = (0, 1, -1)

    barrier = pltpu.get_barrier_semaphore()
    for xi, yi, zi in peers:
        pl.semaphore_signal(barrier, inc=1, device_id=neighbour(xi, yi, shift_z[zi]), device_id_type=MESH)

    row = row_index()
    lane = lax.broadcasted_iota(jnp.int32, (8, LANES), 1)
    slot = lane + LANES * (row % 2)
    occupied = [slot < counts[0, 0, b] for b in range(2)]
    speed = []
    for b in range(2):
        place_rows = [positions[c, 0, 0, b : b + 1, h * LANES : (h + 1) * LANES] for c in range(3) for h in range(2)]
        mass_rows = [mass[0, 0, b : b + 1, h * LANES : (h + 1) * LANES] for h in range(2)]
        packed = jnp.concatenate(place_rows + mass_rows, axis=0)
        bins[0, 0, 1 + b] = jnp.where((row < 6) | occupied[b], packed, 0.0)
        speed_rows = [velocities[c, 0, 0, b : b + 1, h * LANES : (h + 1) * LANES] for c in range(3) for h in range(2)]
        speed.append(jnp.concatenate(speed_rows + [jnp.zeros((2, LANES), jnp.float32)], axis=0))

    pl.semaphore_wait(barrier, len(peers))

    copies = []
    for sub in range(SUBCYCLES):
        for xi, yi, zi in peers:
            from_them = xi * 3 + (3 - yi) % 3
            source = bins.at[sub, 0, pl.ds(1, 2)] if zi == 0 else bins.at[sub, 0, pl.ds(2 if zi == 1 else 1, 1)]
            target = bins.at[sub, from_them, pl.ds(1, 2)] if zi == 0 else bins.at[sub, from_them, pl.ds(0 if zi == 1 else 3, 1)]
            copy = pltpu.make_async_remote_copy(
                src_ref=source,
                dst_ref=target,
                send_sem=send_sem.at[sub, from_them, zi],
                recv_sem=recv_sem.at[sub, from_them, zi],
                device_id=neighbour(xi, yi, shift_z[zi]),
                device_id_type=MESH,
            )
            copy.start()
            copies.append(copy)

        for b in range(2):
            targets[b] = target_features(bins[sub, 0, 1 + b], frame_offset(row, -0.5, -0.5, b - 1.0))
        total[...] = jnp.zeros_like(total)

        def arrived(column, zi):
            width = 2 if zi == 0 else 1
            place = bins.at[sub, column, pl.ds((1, 0, 3)[zi], width)]
            pltpu.make_async_remote_copy(
                src_ref=place,
                dst_ref=place,
                send_sem=send_sem.at[sub, column, zi],
                recv_sem=recv_sem.at[sub, column, zi],
                device_id=neighbour(0, 0, 1),
                device_id_type=MESH,
            ).wait_recv()

        def column_sums(column):
            dx, dy = shift(column // 3, column % 3)
            offset_x = dx.astype(jnp.float32) - 0.5
            offset_y = dy.astype(jnp.float32) - 0.5
            sums = [None, None]
            for z in range(4):
                features, moments = source_features(
                    bins[sub, column, z], frame_offset(row, offset_x, offset_y, z - 2.0)
                )
                for b in range(2):
                    if abs(z - 1 - b) <= 1:
                        value = pair_sums(features, moments, targets[b])
                        sums[b] = value if sums[b] is None else sums[b] + value
            for b in range(2):
                total[b] += sums[b]

        arrived(0, 1)
        arrived(0, 2)
        column_sums(jnp.int32(0))

        def body(column, carry):
            for zi in range(3):
                arrived(column, zi)
            column_sums(column)
            return carry

        lax.fori_loop(1, 9, body, 0)

        for b in range(2):
            packed = bins[sub, 0, 1 + b]
            accel = packed_accel(total[b], packed, frame_offset(row, -0.5, -0.5, b - 1.0))
            speed[b] = speed[b] + time_step * accel
            moved = jnp.clip(packed + time_step * speed[b], 0.0, 1.0)
            if sub + 1 < SUBCYCLES:
                bins[sub + 1, 0, 1 + b] = jnp.where(row < 6, moved, packed)
            else:
                moved = jnp.where(occupied[b], moved, 0.0)
                final_speed = jnp.where(occupied[b], speed[b], 0.0)
                for c in range(3):
                    for h in range(2):
                        r = 2 * c + h
                        new_positions[c, 0, 0, b : b + 1, h * LANES : (h + 1) * LANES] = moved[r : r + 1]
                        new_velocities[c, 0, 0, b : b + 1, h * LANES : (h + 1) * LANES] = final_speed[r : r + 1]

    for copy in copies:
        copy.wait_send()


def solution(mesh):
    placed = (
        P(None, "gx", "gy", "gz", None),
        P(None, "gx", "gy", "gz", None),
        P("gx", "gy", "gz", None),
        P("gx", "gy", "gz"),
    )
    sizes = tuple(mesh.shape[name] for name in ("gx", "gy", "gz"))

    def on_device(positions, velocities, mass, counts):
        vmem = pl.BlockSpec(memory_space=pltpu.VMEM)
        return pl.pallas_call(
            functools.partial(step_kernel, sizes),
            out_shape=(
                jax.ShapeDtypeStruct(positions.shape, jnp.float32),
                jax.ShapeDtypeStruct(velocities.shape, jnp.float32),
            ),
            in_specs=[vmem, vmem, vmem, pl.BlockSpec(memory_space=pltpu.SMEM)],
            out_specs=(vmem, vmem),
            scratch_shapes=[
                pltpu.VMEM((SUBCYCLES, 9, 4, 8, LANES), jnp.float32),
                pltpu.VMEM((2, 32, 4 * LANES), jnp.bfloat16),
                pltpu.VMEM((2, 16, 2 * LANES), jnp.float32),
                pltpu.SemaphoreType.DMA((SUBCYCLES, 9, 3)),
                pltpu.SemaphoreType.DMA((SUBCYCLES, 9, 3)),
            ],
            compiler_params=pltpu.CompilerParams(collective_id=0, has_side_effects=True),
        )(positions, velocities, mass, counts)

    return jax.shard_map(
        on_device,
        mesh=mesh,
        in_specs=placed,
        out_specs=(P(None, "gx", "gy", "gz", None), P(None, "gx", "gy", "gz", None)),
        check_vma=False,
    )
```

```python
import functools

import jax
import jax.numpy as jnp
from jax import lax
from jax.experimental import pallas as pl
from jax.experimental.pallas import tpu as pltpu
from jax.sharding import PartitionSpec as P

SUBCYCLES = 2
LANES = 128
GROUPS = (
    ((0, 1),),
    ((1, 1),),
    ((2, 1), (3, 1), (4, 1), (5, 1), (0, 0), (1, 0)),
    ((6, 1), (7, 1), (8, 1), (2, 0), (3, 0), (4, 0), (5, 0), (6, 0), (7, 0), (8, 0)),
)
time_step = 0.25
MESH = pl.DeviceIdType.MESH


def row_index():
    return lax.broadcasted_iota(jnp.int32, (8, LANES), 0)


def split(value):
    scaled = value * 65537.0
    high = scaled - (scaled - value)
    return high, value - high


def over_components(value):
    value = value + pltpu.roll(value, 2, 0)
    return value + pltpu.roll(value, 4, 0)


def frame_offset(row, offset_x, offset_y, offset_z):
    return jnp.where(row < 2, offset_x, jnp.where(row < 4, offset_y, jnp.where(row < 6, offset_z, 0.0)))


def source_features(packed, offset):
    row = row_index()
    is_mass = row >= 6
    moved = packed + offset
    high, low = split(moved)
    spatial = jnp.where(is_mass, 0.0, moved)
    norm = -over_components(spatial * spatial)
    norm_high, rest = split(norm)
    norm_mid, norm_low = split(rest)
    high = jnp.where(is_mass, 1.0, high)
    low = jnp.where(is_mass, 1.0, low)
    norm_mid, norm_low = pltpu.roll(norm_mid, 2, 0), pltpu.roll(norm_low, 4, 0)
    norms = jnp.where(row < 2, norm_high, jnp.where(row < 4, norm_mid, jnp.where(row < 6, norm_low, 0.0)))
    features = jnp.concatenate([high, low, high, norms], axis=0)
    mass = over_components(jnp.where(is_mass, packed, 0.0))
    moment_high, moment_low = split(mass * jnp.where(is_mass, 1.0, moved))
    even = row % 2 == 0
    moments = jnp.concatenate(
        [
            jnp.concatenate([jnp.where(even, part, 0.0), jnp.where(even, 0.0, part)], axis=1)
            for part in (moment_high, moment_low)
        ],
        axis=0,
    )
    return features.T.astype(jnp.bfloat16), moments.astype(jnp.bfloat16)


def target_features(packed, offset):
    row = row_index()
    is_mass = row >= 6
    even = row % 2 == 0
    moved = jnp.where(is_mass, 0.0, packed + offset)
    sides = [[], []]
    for half in range(2):
        mine = jnp.where(even, moved, pltpu.roll(moved, 1, 0)) if half == 0 else jnp.where(even, pltpu.roll(moved, 7, 0), moved)
        first, rest = split(1.0 - over_components(mine * mine))
        second, third = split(rest)
        high, low = split(2.0 * mine)
        stacked = jnp.concatenate(
            [
                jnp.where(is_mass, first, high),
                jnp.where(is_mass, second, high),
                jnp.where(is_mass, third, low),
                jnp.where(is_mass, 0.0, 1.0),
            ],
            axis=0,
        )
        parity = lax.broadcasted_iota(jnp.int32, (32, LANES), 0) % 2
        for source_half in range(2):
            sides[source_half].append(jnp.where(parity == source_half, stacked, 0.0))
    return jnp.concatenate(sides[0] + sides[1], axis=1).astype(jnp.bfloat16)


def pair_sums(features, moments, targets):
    falloff = jnp.maximum(jnp.dot(features, targets, preferred_element_type=jnp.float32), 0.0)
    weighted = falloff * falloff * falloff
    weighted = jnp.concatenate([weighted[:, : 2 * LANES], weighted[:, 2 * LANES :]], axis=0)
    high = weighted.astype(jnp.bfloat16)
    low = (weighted - high.astype(jnp.float32)).astype(jnp.bfloat16)
    return jnp.dot(moments, high, preferred_element_type=jnp.float32) + jnp.dot(
        moments, low, preferred_element_type=jnp.float32
    )


def packed_accel(total, packed, offset):
    row = row_index()
    even = row % 2 == 0
    folded = total[:8] + total[8:]
    halves = []
    for half in range(2):
        part = folded[:, half * LANES : (half + 1) * LANES]
        halves.append(jnp.where(even, part + pltpu.roll(part, 7, 0), part + pltpu.roll(part, 1, 0)))
    sums = jnp.where(even, halves[0], halves[1])
    mass_sum = over_components(jnp.where(row >= 6, sums, 0.0))
    return jnp.where(row >= 6, 0.0, sums - (packed + offset) * mass_sum)


def step_kernel(
    sizes,
    positions,
    velocities,
    mass,
    counts,
    moved_out,
    place_in,
    speed_in,
    mass_in,
    count_in,
    bins,
    targets,
    total,
    input_sem,
    send_sem,
    recv_sem,
):
    inputs = [
        pltpu.make_async_copy(source, target, input_sem.at[i])
        for i, (source, target) in enumerate(
            ((positions, place_in), (mass, mass_in), (counts, count_in), (velocities, speed_in))
        )
    ]
    for load in inputs:
        load.start()

    me = [lax.axis_index(name) for name in ("gx", "gy", "gz")]
    near = 1 - 2 * (me[0] % 2)
    shift_z = (0, 1, -1)

    def neighbour(xi, yi, zi):
        dx = near * (xi % 2) - near * (xi // 2)
        dy = (yi % 2) - (yi // 2)
        return tuple(lax.rem(at + d + size, size) for at, d, size in zip(me, (dx, dy, shift_z[zi]), sizes))

    order = ((0, 0), (1, 0), (0, 1), (0, 2), (1, 1), (1, 2), (2, 1), (2, 2), (2, 0))
    peers = [(xi, yi, zi) for xi, yi in reversed(order) for zi in range(3) if (xi, yi, zi) != (0, 0, 0)]

    barrier = pltpu.get_barrier_semaphore()
    for peer in peers:
        pl.semaphore_signal(barrier, inc=1, device_id=neighbour(*peer), device_id_type=MESH)

    row = row_index()
    lane = lax.broadcasted_iota(jnp.int32, (8, LANES), 1)
    slot = lane + LANES * (row % 2)
    own_offset = [frame_offset(row, -0.5, -0.5, b - 1.0) for b in range(2)]
    for load in inputs:
        load.wait()
    speed = []
    for b in range(2):
        place_rows = [place_in[c, 0, 0, b : b + 1, h * LANES : (h + 1) * LANES] for c in range(3) for h in range(2)]
        mass_rows = [mass_in[0, 0, b : b + 1, h * LANES : (h + 1) * LANES] for h in range(2)]
        packed = jnp.concatenate(place_rows + mass_rows, axis=0)
        bins[0, 0, 1 + b] = jnp.where((row < 6) | (slot < count_in[0, 0, b]), packed, 0.0)
        speed_rows = [speed_in[c, 0, 0, b : b + 1, h * LANES : (h + 1) * LANES] for c in range(3) for h in range(2)]
        speed.append(jnp.concatenate(speed_rows + [jnp.zeros((2, LANES), jnp.float32)], axis=0))

    copies = []
    for sub in range(SUBCYCLES):

        def send():
            for xi, yi, zi in peers:
                column = order.index((xi, (3 - yi) % 3))
                source = bins.at[sub, 0, pl.ds((1, 2, 1)[zi], 2 if zi == 0 else 1)]
                target = bins.at[sub, column, pl.ds((1, 0, 3)[zi], 2 if zi == 0 else 1)]
                copy = pltpu.make_async_remote_copy(
                    src_ref=source,
                    dst_ref=target,
                    send_sem=send_sem.at[sub, column, zi],
                    recv_sem=recv_sem.at[sub, column, zi],
                    device_id=neighbour(xi, yi, zi),
                    device_id_type=MESH,
                )
                copy.start()
                copies.append(copy)

        def arrived(column, zi):
            place = bins.at[sub, column, pl.ds((1, 0, 3)[zi], 2 if zi == 0 else 1)]
            pltpu.make_async_remote_copy(
                src_ref=place,
                dst_ref=place,
                send_sem=send_sem.at[sub, column, zi],
                recv_sem=recv_sem.at[sub, column, zi],
                device_id=neighbour(0, 0, 1),
                device_id_type=MESH,
            ).wait_recv()

        def column_sums(column, slots, sums):
            xi, yi = order[column]
            offset_x = (near * (xi % 2) - near * (xi // 2)).astype(jnp.float32) - 0.5 if xi else -0.5
            offset_y = float((yi % 2) - (yi // 2)) - 0.5
            sums = list(sums)
            for z in slots:
                features, moments = source_features(
                    bins[sub, column, z], frame_offset(row, offset_x, offset_y, z - 2.0)
                )
                for b in range(2):
                    if abs(z - 1 - b) <= 1:
                        value = pair_sums(features, moments, targets[b])
                        sums[b] = value if sums[b] is None else sums[b] + value
            return sums

        def accumulate(group):
            for column, inner in group:
                for zi in (0,) if inner else (1, 2):
                    if (column, zi) != (0, 0):
                        arrived(column, zi)
            sums = [None, None]
            for column, inner in group:
                sums = column_sums(column, (1, 2) if inner else (0, 3), sums)
            for b in range(2):
                total[b] += sums[b]

        if sub == 0:
            for b in range(2):
                targets[b] = target_features(bins[sub, 0, 1 + b], own_offset[b])
            total[...] = jnp.zeros_like(total)
            pl.semaphore_wait(barrier, len(peers))
            send()
        else:
            send()
            for b in range(2):
                targets[b] = target_features(bins[sub, 0, 1 + b], own_offset[b])
            total[...] = jnp.zeros_like(total)

        for group in GROUPS:
            accumulate(group)

        for b in range(2):
            packed = bins[sub, 0, 1 + b]
            accel = packed_accel(total[b], packed, own_offset[b])
            speed[b] = speed[b] + time_step * accel
            moved = jnp.clip(packed + time_step * speed[b], 0.0, 1.0)
            if sub + 1 < SUBCYCLES:
                bins[sub + 1, 0, 1 + b] = jnp.where(row < 6, moved, packed)
            else:
                occupied = slot < count_in[0, 0, b]
                moved = jnp.where(occupied, moved, 0.0)
                final_speed = jnp.where(occupied, speed[b], 0.0)
                for c in range(3):
                    for h in range(2):
                        r = 2 * c + h
                        moved_out[c, 0, 0, b : b + 1, h * LANES : (h + 1) * LANES] = moved[r : r + 1]
                        moved_out[3 + c, 0, 0, b : b + 1, h * LANES : (h + 1) * LANES] = final_speed[r : r + 1]

    for copy in copies:
        copy.wait_send()


def solution(mesh):
    placed = (
        P(None, "gx", "gy", "gz", None),
        P(None, "gx", "gy", "gz", None),
        P("gx", "gy", "gz", None),
        P("gx", "gy", "gz"),
    )
    sizes = tuple(mesh.shape[name] for name in ("gx", "gy", "gz"))

    def on_device(positions, velocities, mass, counts):
        anywhere = pl.BlockSpec(memory_space=pl.ANY)
        moved = pl.pallas_call(
            functools.partial(step_kernel, sizes),
            out_shape=jax.ShapeDtypeStruct((6,) + positions.shape[1:], jnp.float32),
            in_specs=[anywhere] * 4,
            out_specs=pl.BlockSpec(memory_space=pltpu.VMEM),
            scratch_shapes=[
                pltpu.VMEM(positions.shape, jnp.float32),
                pltpu.VMEM(velocities.shape, jnp.float32),
                pltpu.VMEM(mass.shape, jnp.float32),
                pltpu.SMEM(counts.shape, jnp.int32),
                pltpu.VMEM((SUBCYCLES, 9, 4, 8, LANES), jnp.float32),
                pltpu.VMEM((2, 32, 4 * LANES), jnp.bfloat16),
                pltpu.VMEM((2, 16, 2 * LANES), jnp.float32),
                pltpu.SemaphoreType.DMA((4,)),
                pltpu.SemaphoreType.DMA((SUBCYCLES, 9, 3)),
                pltpu.SemaphoreType.DMA((SUBCYCLES, 9, 3)),
            ],
            compiler_params=pltpu.CompilerParams(collective_id=0, has_side_effects=True),
        )(positions, velocities, mass, counts)
        return moved[:3], moved[3:]

    return jax.shard_map(
        on_device,
        mesh=mesh,
        in_specs=placed,
        out_specs=(P(None, "gx", "gy", "gz", None), P(None, "gx", "gy", "gz", None)),
        check_vma=False,
    )
```

```python
import functools

import jax
import jax.numpy as jnp
from jax import lax
from jax.experimental import pallas as pl
from jax.experimental.pallas import tpu as pltpu
from jax.sharding import PartitionSpec as P

SUBCYCLES = 2
LANES = 128
GROUPS = (
    ((0, 1),),
    ((1, 1), (2, 1), (3, 1), (4, 1), (5, 1), (0, 0), (1, 0)),
    ((6, 1), (7, 1), (8, 1), (2, 0), (3, 0), (4, 0), (5, 0), (6, 0), (7, 0), (8, 0)),
)
time_step = 0.25
MESH = pl.DeviceIdType.MESH


def row_index():
    return lax.broadcasted_iota(jnp.int32, (8, LANES), 0)


def split(value):
    scaled = value * 65537.0
    high = scaled - (scaled - value)
    return high, value - high


def over_components(value):
    value = value + pltpu.roll(value, 2, 0)
    return value + pltpu.roll(value, 4, 0)


def frame_offset(row, offset_x, offset_y, offset_z):
    return jnp.where(row < 2, offset_x, jnp.where(row < 4, offset_y, jnp.where(row < 6, offset_z, 0.0)))


def source_features(packed, offset):
    row = row_index()
    is_mass = row >= 6
    moved = packed + offset
    high, low = split(moved)
    spatial = jnp.where(is_mass, 0.0, moved)
    norm = -over_components(spatial * spatial)
    norm_high, rest = split(norm)
    norm_mid, norm_low = split(rest)
    high = jnp.where(is_mass, 1.0, high)
    low = jnp.where(is_mass, 1.0, low)
    norm_mid, norm_low = pltpu.roll(norm_mid, 2, 0), pltpu.roll(norm_low, 4, 0)
    norms = jnp.where(row < 2, norm_high, jnp.where(row < 4, norm_mid, jnp.where(row < 6, norm_low, 0.0)))
    features = jnp.concatenate([high, low, high, norms], axis=0)
    mass = over_components(jnp.where(is_mass, packed, 0.0))
    moment_high, moment_low = split(mass * jnp.where(is_mass, 1.0, moved))
    even = row % 2 == 0
    moments = jnp.concatenate(
        [
            jnp.concatenate([jnp.where(even, part, 0.0), jnp.where(even, 0.0, part)], axis=1)
            for part in (moment_high, moment_low)
        ],
        axis=0,
    )
    return features.T.astype(jnp.bfloat16), moments.astype(jnp.bfloat16)


def target_features(packed, offset):
    row = row_index()
    is_mass = row >= 6
    even = row % 2 == 0
    moved = jnp.where(is_mass, 0.0, packed + offset)
    sides = [[], []]
    for half in range(2):
        mine = jnp.where(even, moved, pltpu.roll(moved, 1, 0)) if half == 0 else jnp.where(even, pltpu.roll(moved, 7, 0), moved)
        first, rest = split(1.0 - over_components(mine * mine))
        second, third = split(rest)
        high, low = split(2.0 * mine)
        stacked = jnp.concatenate(
            [
                jnp.where(is_mass, first, high),
                jnp.where(is_mass, second, high),
                jnp.where(is_mass, third, low),
                jnp.where(is_mass, 0.0, 1.0),
            ],
            axis=0,
        )
        parity = lax.broadcasted_iota(jnp.int32, (32, LANES), 0) % 2
        for source_half in range(2):
            sides[source_half].append(jnp.where(parity == source_half, stacked, 0.0))
    return jnp.concatenate(sides[0] + sides[1], axis=1).astype(jnp.bfloat16)


def pair_sums(features, moments, targets):
    falloff = jnp.maximum(jnp.dot(features, targets, preferred_element_type=jnp.float32), 0.0)
    weighted = falloff * falloff * falloff
    weighted = jnp.concatenate([weighted[:, : 2 * LANES], weighted[:, 2 * LANES :]], axis=0)
    high = weighted.astype(jnp.bfloat16)
    low = (weighted - high.astype(jnp.float32)).astype(jnp.bfloat16)
    return jnp.dot(moments, high, preferred_element_type=jnp.float32) + jnp.dot(
        moments, low, preferred_element_type=jnp.float32
    )


def packed_accel(total, packed, offset):
    row = row_index()
    even = row % 2 == 0
    folded = total[:8] + total[8:]
    halves = []
    for half in range(2):
        part = folded[:, half * LANES : (half + 1) * LANES]
        halves.append(jnp.where(even, part + pltpu.roll(part, 7, 0), part + pltpu.roll(part, 1, 0)))
    sums = jnp.where(even, halves[0], halves[1])
    mass_sum = over_components(jnp.where(row >= 6, sums, 0.0))
    return jnp.where(row >= 6, 0.0, sums - (packed + offset) * mass_sum)


def step_kernel(
    sizes,
    positions,
    velocities,
    mass,
    counts,
    moved_out,
    place_in,
    speed_in,
    mass_in,
    count_in,
    bins,
    targets,
    total,
    input_sem,
    send_sem,
    recv_sem,
):
    inputs = [
        pltpu.make_async_copy(source, target, input_sem.at[i])
        for i, (source, target) in enumerate(
            ((positions, place_in), (mass, mass_in), (counts, count_in), (velocities, speed_in))
        )
    ]
    for load in inputs:
        load.start()

    me = [lax.axis_index(name) for name in ("gx", "gy", "gz")]
    near = 1 - 2 * (me[0] % 2)
    shift_z = (0, 1, -1)

    def neighbour(xi, yi, zi):
        dx = near * (xi % 2) - near * (xi // 2)
        dy = (yi % 2) - (yi // 2)
        return tuple(lax.rem(at + d + size, size) for at, d, size in zip(me, (dx, dy, shift_z[zi]), sizes))

    order = ((0, 0), (1, 0), (0, 1), (0, 2), (1, 1), (1, 2), (2, 1), (2, 2), (2, 0))
    peers = [(xi, yi, zi) for xi, yi in reversed(order) for zi in range(3) if (xi, yi, zi) != (0, 0, 0)]

    barrier = pltpu.get_barrier_semaphore()
    for peer in peers:
        pl.semaphore_signal(barrier, inc=1, device_id=neighbour(*peer), device_id_type=MESH)

    row = row_index()
    lane = lax.broadcasted_iota(jnp.int32, (8, LANES), 1)
    slot = lane + LANES * (row % 2)
    own_offset = [frame_offset(row, -0.5, -0.5, b - 1.0) for b in range(2)]
    for load in inputs:
        load.wait()
    speed = []
    for b in range(2):
        place_rows = [place_in[c, 0, 0, b : b + 1, h * LANES : (h + 1) * LANES] for c in range(3) for h in range(2)]
        mass_rows = [mass_in[0, 0, b : b + 1, h * LANES : (h + 1) * LANES] for h in range(2)]
        packed = jnp.concatenate(place_rows + mass_rows, axis=0)
        bins[0, 0, 1 + b] = jnp.where((row < 6) | (slot < count_in[0, 0, b]), packed, 0.0)
        speed_rows = [speed_in[c, 0, 0, b : b + 1, h * LANES : (h + 1) * LANES] for c in range(3) for h in range(2)]
        speed.append(jnp.concatenate(speed_rows + [jnp.zeros((2, LANES), jnp.float32)], axis=0))

    copies = []
    for sub in range(SUBCYCLES):

        def send():
            for xi, yi, zi in peers:
                column = order.index((xi, (3 - yi) % 3))
                source = bins.at[sub, 0, pl.ds((1, 2, 1)[zi], 2 if zi == 0 else 1)]
                target = bins.at[sub, column, pl.ds((1, 0, 3)[zi], 2 if zi == 0 else 1)]
                copy = pltpu.make_async_remote_copy(
                    src_ref=source,
                    dst_ref=target,
                    send_sem=send_sem.at[sub, column, zi],
                    recv_sem=recv_sem.at[sub, column, zi],
                    device_id=neighbour(xi, yi, zi),
                    device_id_type=MESH,
                )
                copy.start()
                copies.append(copy)

        def arrived(column, zi):
            place = bins.at[sub, column, pl.ds((1, 0, 3)[zi], 2 if zi == 0 else 1)]
            pltpu.make_async_remote_copy(
                src_ref=place,
                dst_ref=place,
                send_sem=send_sem.at[sub, column, zi],
                recv_sem=recv_sem.at[sub, column, zi],
                device_id=neighbour(0, 0, 1),
                device_id_type=MESH,
            ).wait_recv()

        def column_sums(column, slots, sums):
            xi, yi = order[column]
            offset_x = (near * (xi % 2) - near * (xi // 2)).astype(jnp.float32) - 0.5 if xi else -0.5
            offset_y = float((yi % 2) - (yi // 2)) - 0.5
            sums = list(sums)
            for z in slots:
                features, moments = source_features(
                    bins[sub, column, z], frame_offset(row, offset_x, offset_y, z - 2.0)
                )
                for b in range(2):
                    if abs(z - 1 - b) <= 1:
                        value = pair_sums(features, moments, targets[b])
                        sums[b] = value if sums[b] is None else sums[b] + value
            return sums

        def accumulate(group):
            for column, inner in group:
                for zi in (0,) if inner else (1, 2):
                    if (column, zi) != (0, 0):
                        arrived(column, zi)
            sums = [None, None]
            for column, inner in group:
                sums = column_sums(column, (1, 2) if inner else (0, 3), sums)
            for b in range(2):
                total[b] += sums[b]

        if sub == 0:
            for b in range(2):
                targets[b] = target_features(bins[sub, 0, 1 + b], own_offset[b])
            total[...] = jnp.zeros_like(total)
            accumulate(GROUPS[0])
            pl.semaphore_wait(barrier, len(peers))
            send()
        else:
            send()
            for b in range(2):
                targets[b] = target_features(bins[sub, 0, 1 + b], own_offset[b])
            total[...] = jnp.zeros_like(total)
            accumulate(GROUPS[0])

        for group in GROUPS[1:]:
            accumulate(group)

        for b in range(2):
            packed = bins[sub, 0, 1 + b]
            accel = packed_accel(total[b], packed, own_offset[b])
            speed[b] = speed[b] + time_step * accel
            moved = jnp.clip(packed + time_step * speed[b], 0.0, 1.0)
            if sub + 1 < SUBCYCLES:
                bins[sub + 1, 0, 1 + b] = jnp.where(row < 6, moved, packed)
            else:
                occupied = slot < count_in[0, 0, b]
                moved = jnp.where(occupied, moved, 0.0)
                final_speed = jnp.where(occupied, speed[b], 0.0)
                for c in range(3):
                    for h in range(2):
                        r = 2 * c + h
                        moved_out[c, 0, 0, b : b + 1, h * LANES : (h + 1) * LANES] = moved[r : r + 1]
                        moved_out[3 + c, 0, 0, b : b + 1, h * LANES : (h + 1) * LANES] = final_speed[r : r + 1]

    for copy in copies:
        copy.wait_send()


def solution(mesh):
    placed = (
        P(None, "gx", "gy", "gz", None),
        P(None, "gx", "gy", "gz", None),
        P("gx", "gy", "gz", None),
        P("gx", "gy", "gz"),
    )
    sizes = tuple(mesh.shape[name] for name in ("gx", "gy", "gz"))

    def on_device(positions, velocities, mass, counts):
        anywhere = pl.BlockSpec(memory_space=pl.ANY)
        moved = pl.pallas_call(
            functools.partial(step_kernel, sizes),
            out_shape=pltpu.VMEM((6,) + positions.shape[1:], jnp.float32),
            in_specs=[anywhere] * 4,
            out_specs=pl.BlockSpec(memory_space=pltpu.VMEM),
            scratch_shapes=[
                pltpu.VMEM(positions.shape, jnp.float32),
                pltpu.VMEM(velocities.shape, jnp.float32),
                pltpu.VMEM(mass.shape, jnp.float32),
                pltpu.SMEM(counts.shape, jnp.int32),
                pltpu.VMEM((SUBCYCLES, 9, 4, 8, LANES), jnp.float32),
                pltpu.VMEM((2, 32, 4 * LANES), jnp.bfloat16),
                pltpu.VMEM((2, 16, 2 * LANES), jnp.float32),
                pltpu.SemaphoreType.DMA((4,)),
                pltpu.SemaphoreType.DMA((SUBCYCLES, 9, 3)),
                pltpu.SemaphoreType.DMA((SUBCYCLES, 9, 3)),
            ],
            compiler_params=pltpu.CompilerParams(collective_id=0, has_side_effects=True),
        )(positions, velocities, mass, counts)
        return moved[:3], moved[3:]

    return jax.shard_map(
        on_device,
        mesh=mesh,
        in_specs=placed,
        out_specs=(P(None, "gx", "gy", "gz", None), P(None, "gx", "gy", "gz", None)),
        check_vma=False,
    )
```

```python
import functools

import jax
import jax.numpy as jnp
from jax import lax
from jax.experimental import pallas as pl
from jax.experimental.pallas import tpu as pltpu
from jax.sharding import PartitionSpec as P

SUBCYCLES = 2
LANES = 128
GROUPS = (
    ((0, 1),),
    ((1, 1), (2, 1), (3, 1), (4, 1), (5, 1), (0, 0), (1, 0)),
    ((6, 1), (7, 1), (8, 1), (2, 0), (3, 0), (4, 0), (5, 0), (6, 0), (7, 0), (8, 0)),
)
time_step = 0.25
MESH = pl.DeviceIdType.MESH


def row_index():
    return lax.broadcasted_iota(jnp.int32, (8, LANES), 0)


def split(value):
    scaled = value * 65537.0
    high = scaled - (scaled - value)
    return high, value - high


def over_components(value):
    value = value + pltpu.roll(value, 2, 0)
    return value + pltpu.roll(value, 4, 0)


def frame_offset(row, offset_x, offset_y, offset_z):
    return jnp.where(row < 2, offset_x, jnp.where(row < 4, offset_y, jnp.where(row < 6, offset_z, 0.0)))


def source_features(packed, offset):
    row = row_index()
    is_mass = row >= 6
    moved = packed + offset
    high, low = split(moved)
    spatial = jnp.where(is_mass, 0.0, moved)
    norm = -over_components(spatial * spatial)
    norm_high, rest = split(norm)
    norm_mid, norm_low = split(rest)
    high = jnp.where(is_mass, 1.0, high)
    low = jnp.where(is_mass, 1.0, low)
    norm_mid, norm_low = pltpu.roll(norm_mid, 2, 0), pltpu.roll(norm_low, 4, 0)
    norms = jnp.where(row < 2, norm_high, jnp.where(row < 4, norm_mid, jnp.where(row < 6, norm_low, 0.0)))
    features = jnp.concatenate([high, low, high, norms], axis=0)
    mass = over_components(jnp.where(is_mass, packed, 0.0))
    moment_high, moment_low = split(mass * jnp.where(is_mass, 1.0, moved))
    even = row % 2 == 0
    moments = jnp.concatenate(
        [
            jnp.concatenate([jnp.where(even, part, 0.0), jnp.where(even, 0.0, part)], axis=1)
            for part in (moment_high, moment_low)
        ],
        axis=0,
    )
    return features.T.astype(jnp.bfloat16), moments.astype(jnp.bfloat16)


def target_features(packed, offset):
    row = row_index()
    is_mass = row >= 6
    even = row % 2 == 0
    moved = jnp.where(is_mass, 0.0, packed + offset)
    sides = [[], []]
    for half in range(2):
        mine = jnp.where(even, moved, pltpu.roll(moved, 1, 0)) if half == 0 else jnp.where(even, pltpu.roll(moved, 7, 0), moved)
        first, rest = split(1.0 - over_components(mine * mine))
        second, third = split(rest)
        high, low = split(2.0 * mine)
        stacked = jnp.concatenate(
            [
                jnp.where(is_mass, first, high),
                jnp.where(is_mass, second, high),
                jnp.where(is_mass, third, low),
                jnp.where(is_mass, 0.0, 1.0),
            ],
            axis=0,
        )
        parity = lax.broadcasted_iota(jnp.int32, (32, LANES), 0) % 2
        for source_half in range(2):
            sides[source_half].append(jnp.where(parity == source_half, stacked, 0.0))
    return jnp.concatenate(sides[0] + sides[1], axis=1).astype(jnp.bfloat16)


def pair_sums(features, moments, targets):
    falloff = jnp.maximum(jnp.dot(features, targets, preferred_element_type=jnp.float32), 0.0)
    weighted = falloff * falloff * falloff
    weighted = jnp.concatenate([weighted[:, : 2 * LANES], weighted[:, 2 * LANES :]], axis=0)
    high = weighted.astype(jnp.bfloat16)
    low = (weighted - high.astype(jnp.float32)).astype(jnp.bfloat16)
    return jnp.dot(moments, high, preferred_element_type=jnp.float32) + jnp.dot(
        moments, low, preferred_element_type=jnp.float32
    )


def packed_accel(total, packed, offset):
    row = row_index()
    even = row % 2 == 0
    folded = total[:8] + total[8:]
    halves = []
    for half in range(2):
        part = folded[:, half * LANES : (half + 1) * LANES]
        halves.append(jnp.where(even, part + pltpu.roll(part, 7, 0), part + pltpu.roll(part, 1, 0)))
    sums = jnp.where(even, halves[0], halves[1])
    mass_sum = over_components(jnp.where(row >= 6, sums, 0.0))
    return jnp.where(row >= 6, 0.0, sums - (packed + offset) * mass_sum)


def step_kernel(
    sizes,
    positions,
    velocities,
    mass,
    counts,
    moved_out,
    place_in,
    speed_in,
    mass_in,
    count_in,
    bins,
    targets,
    total,
    input_sem,
    send_sem,
    recv_sem,
):
    inputs = [
        pltpu.make_async_copy(source, target, input_sem.at[i])
        for i, (source, target) in enumerate(
            ((positions, place_in), (mass, mass_in), (counts, count_in), (velocities, speed_in))
        )
    ]
    for load in inputs:
        load.start()

    me = [lax.axis_index(name) for name in ("gx", "gy", "gz")]
    near = 1 - 2 * (me[0] % 2)
    shift_z = (0, 1, -1)

    def neighbour(xi, yi, zi):
        dx = near * (xi % 2) - near * (xi // 2)
        dy = (yi % 2) - (yi // 2)
        return tuple(lax.rem(at + d + size, size) for at, d, size in zip(me, (dx, dy, shift_z[zi]), sizes))

    order = ((0, 0), (1, 0), (0, 1), (0, 2), (1, 1), (1, 2), (2, 1), (2, 2), (2, 0))
    peers = [(xi, yi, zi) for xi, yi in reversed(order) for zi in range(3) if (xi, yi, zi) != (0, 0, 0)]

    barrier = pltpu.get_barrier_semaphore()
    for peer in peers:
        pl.semaphore_signal(barrier, inc=1, device_id=neighbour(*peer), device_id_type=MESH)

    row = row_index()
    lane = lax.broadcasted_iota(jnp.int32, (8, LANES), 1)
    slot = lane + LANES * (row % 2)
    own_offset = [frame_offset(row, -0.5, -0.5, b - 1.0) for b in range(2)]
    for load in inputs:
        load.wait()
    speed = []
    for b in range(2):
        place_rows = [place_in[c, 0, 0, b : b + 1, h * LANES : (h + 1) * LANES] for c in range(3) for h in range(2)]
        mass_rows = [mass_in[0, 0, b : b + 1, h * LANES : (h + 1) * LANES] for h in range(2)]
        packed = jnp.concatenate(place_rows + mass_rows, axis=0)
        bins[0, 0, 1 + b] = jnp.where((row < 6) | (slot < count_in[0, 0, b]), packed, 0.0)
        speed_rows = [speed_in[c, 0, 0, b : b + 1, h * LANES : (h + 1) * LANES] for c in range(3) for h in range(2)]
        speed.append(jnp.concatenate(speed_rows + [jnp.zeros((2, LANES), jnp.float32)], axis=0))

    copies = []
    for sub in range(SUBCYCLES):

        def send():
            for xi, yi, zi in peers:
                column = order.index((xi, (3 - yi) % 3))
                rows = pl.ds(0, 8 if sub == 0 else 6)
                source = bins.at[sub, 0, pl.ds((1, 2, 1)[zi], 2 if zi == 0 else 1), rows]
                target = bins.at[sub, column, pl.ds((1, 0, 3)[zi], 2 if zi == 0 else 1), rows]
                copy = pltpu.make_async_remote_copy(
                    src_ref=source,
                    dst_ref=target,
                    send_sem=send_sem.at[sub, column, zi],
                    recv_sem=recv_sem.at[sub, column, zi],
                    device_id=neighbour(xi, yi, zi),
                    device_id_type=MESH,
                )
                copy.start()
                copies.append(copy)

        def arrived(column, zi):
            place = bins.at[sub, column, pl.ds((1, 0, 3)[zi], 2 if zi == 0 else 1), pl.ds(0, 8 if sub == 0 else 6)]
            pltpu.make_async_remote_copy(
                src_ref=place,
                dst_ref=place,
                send_sem=send_sem.at[sub, column, zi],
                recv_sem=recv_sem.at[sub, column, zi],
                device_id=neighbour(0, 0, 1),
                device_id_type=MESH,
            ).wait_recv()

        def column_sums(column, slots, sums):
            xi, yi = order[column]
            offset_x = (near * (xi % 2) - near * (xi // 2)).astype(jnp.float32) - 0.5 if xi else -0.5
            offset_y = float((yi % 2) - (yi // 2)) - 0.5
            sums = list(sums)
            for z in slots:
                packed = bins[sub, column, z]
                if sub > 0:
                    packed = jnp.where(row < 6, packed, bins[0, column, z])
                features, moments = source_features(packed, frame_offset(row, offset_x, offset_y, z - 2.0))
                for b in range(2):
                    if abs(z - 1 - b) <= 1:
                        value = pair_sums(features, moments, targets[b])
                        sums[b] = value if sums[b] is None else sums[b] + value
            return sums

        def accumulate(group):
            for column, inner in group:
                for zi in (0,) if inner else (1, 2):
                    if (column, zi) != (0, 0):
                        arrived(column, zi)
            sums = [None, None]
            for column, inner in group:
                sums = column_sums(column, (1, 2) if inner else (0, 3), sums)
            for b in range(2):
                total[b] += sums[b]

        if sub == 0:
            for b in range(2):
                targets[b] = target_features(bins[sub, 0, 1 + b], own_offset[b])
            total[...] = jnp.zeros_like(total)
            accumulate(GROUPS[0])
            pl.semaphore_wait(barrier, len(peers))
            send()
        else:
            send()
            for b in range(2):
                targets[b] = target_features(bins[sub, 0, 1 + b], own_offset[b])
            total[...] = jnp.zeros_like(total)
            accumulate(GROUPS[0])

        for group in GROUPS[1:]:
            accumulate(group)

        for b in range(2):
            packed = bins[sub, 0, 1 + b]
            accel = packed_accel(total[b], packed, own_offset[b])
            speed[b] = speed[b] + time_step * accel
            moved = jnp.clip(packed + time_step * speed[b], 0.0, 1.0)
            if sub + 1 < SUBCYCLES:
                bins[sub + 1, 0, 1 + b] = jnp.where(row < 6, moved, packed)
            else:
                occupied = slot < count_in[0, 0, b]
                moved = jnp.where(occupied, moved, 0.0)
                final_speed = jnp.where(occupied, speed[b], 0.0)
                for c in range(3):
                    for h in range(2):
                        r = 2 * c + h
                        moved_out[c, 0, 0, b : b + 1, h * LANES : (h + 1) * LANES] = moved[r : r + 1]
                        moved_out[3 + c, 0, 0, b : b + 1, h * LANES : (h + 1) * LANES] = final_speed[r : r + 1]

    for copy in copies:
        copy.wait_send()


def solution(mesh):
    placed = (
        P(None, "gx", "gy", "gz", None),
        P(None, "gx", "gy", "gz", None),
        P("gx", "gy", "gz", None),
        P("gx", "gy", "gz"),
    )
    sizes = tuple(mesh.shape[name] for name in ("gx", "gy", "gz"))

    def on_device(positions, velocities, mass, counts):
        anywhere = pl.BlockSpec(memory_space=pl.ANY)
        moved = pl.pallas_call(
            functools.partial(step_kernel, sizes),
            out_shape=pltpu.VMEM((6,) + positions.shape[1:], jnp.float32),
            in_specs=[anywhere] * 4,
            out_specs=pl.BlockSpec(memory_space=pltpu.VMEM),
            scratch_shapes=[
                pltpu.VMEM(positions.shape, jnp.float32),
                pltpu.VMEM(velocities.shape, jnp.float32),
                pltpu.VMEM(mass.shape, jnp.float32),
                pltpu.SMEM(counts.shape, jnp.int32),
                pltpu.VMEM((SUBCYCLES, 9, 4, 8, LANES), jnp.float32),
                pltpu.VMEM((2, 32, 4 * LANES), jnp.bfloat16),
                pltpu.VMEM((2, 16, 2 * LANES), jnp.float32),
                pltpu.SemaphoreType.DMA((4,)),
                pltpu.SemaphoreType.DMA((SUBCYCLES, 9, 3)),
                pltpu.SemaphoreType.DMA((SUBCYCLES, 9, 3)),
            ],
            compiler_params=pltpu.CompilerParams(collective_id=0, has_side_effects=True),
        )(positions, velocities, mass, counts)
        return moved[:3], moved[3:]

    return jax.shard_map(
        on_device,
        mesh=mesh,
        in_specs=placed,
        out_specs=(P(None, "gx", "gy", "gz", None), P(None, "gx", "gy", "gz", None)),
        check_vma=False,
    )
```

```python
import functools

import jax
import jax.numpy as jnp
from jax import lax
from jax.experimental import pallas as pl
from jax.experimental.pallas import tpu as pltpu
from jax.sharding import PartitionSpec as P

SUBCYCLES = 2
LANES = 128
GROUPS = (
    ((0, 1),),
    ((1, 1), (2, 1), (3, 1)),
    ((4, 1), (5, 1), (0, 0), (1, 0), (2, 0), (3, 0)),
    ((6, 1), (7, 1), (8, 1), (4, 0), (5, 0), (6, 0), (7, 0), (8, 0)),
)
time_step = 0.25
MESH = pl.DeviceIdType.MESH


def row_index():
    return lax.broadcasted_iota(jnp.int32, (8, LANES), 0)


def split(value):
    scaled = value * 65537.0
    high = scaled - (scaled - value)
    return high, value - high


def over_components(value):
    value = value + pltpu.roll(value, 2, 0)
    return value + pltpu.roll(value, 4, 0)


def frame_offset(row, offset_x, offset_y, offset_z):
    return jnp.where(row < 2, offset_x, jnp.where(row < 4, offset_y, jnp.where(row < 6, offset_z, 0.0)))


def source_features(packed, offset):
    row = row_index()
    is_mass = row >= 6
    moved = packed + offset
    high, low = split(moved)
    spatial = jnp.where(is_mass, 0.0, moved)
    norm = -over_components(spatial * spatial)
    norm_high, rest = split(norm)
    norm_mid, norm_low = split(rest)
    high = jnp.where(is_mass, 1.0, high)
    low = jnp.where(is_mass, 1.0, low)
    norm_mid, norm_low = pltpu.roll(norm_mid, 2, 0), pltpu.roll(norm_low, 4, 0)
    norms = jnp.where(row < 2, norm_high, jnp.where(row < 4, norm_mid, jnp.where(row < 6, norm_low, 0.0)))
    features = jnp.concatenate([high, low, high, norms], axis=0)
    mass = over_components(jnp.where(is_mass, packed, 0.0))
    moment_high, moment_low = split(mass * jnp.where(is_mass, 1.0, moved))
    even = row % 2 == 0
    moments = jnp.concatenate(
        [
            jnp.concatenate([jnp.where(even, part, 0.0), jnp.where(even, 0.0, part)], axis=1)
            for part in (moment_high, moment_low)
        ],
        axis=0,
    )
    return features.T.astype(jnp.bfloat16), moments.astype(jnp.bfloat16)


def target_features(packed, offset):
    row = row_index()
    is_mass = row >= 6
    even = row % 2 == 0
    moved = jnp.where(is_mass, 0.0, packed + offset)
    sides = [[], []]
    for half in range(2):
        mine = jnp.where(even, moved, pltpu.roll(moved, 1, 0)) if half == 0 else jnp.where(even, pltpu.roll(moved, 7, 0), moved)
        first, rest = split(1.0 - over_components(mine * mine))
        second, third = split(rest)
        high, low = split(2.0 * mine)
        stacked = jnp.concatenate(
            [
                jnp.where(is_mass, first, high),
                jnp.where(is_mass, second, high),
                jnp.where(is_mass, third, low),
                jnp.where(is_mass, 0.0, 1.0),
            ],
            axis=0,
        )
        parity = lax.broadcasted_iota(jnp.int32, (32, LANES), 0) % 2
        for source_half in range(2):
            sides[source_half].append(jnp.where(parity == source_half, stacked, 0.0))
    return jnp.concatenate(sides[0] + sides[1], axis=1).astype(jnp.bfloat16)


def pair_sums(features, moments, targets):
    falloff = jnp.maximum(jnp.dot(features, targets, preferred_element_type=jnp.float32), 0.0)
    weighted = falloff * falloff * falloff
    weighted = jnp.concatenate([weighted[:, : 2 * LANES], weighted[:, 2 * LANES :]], axis=0)
    high = weighted.astype(jnp.bfloat16)
    low = (weighted - high.astype(jnp.float32)).astype(jnp.bfloat16)
    return jnp.dot(moments, high, preferred_element_type=jnp.float32) + jnp.dot(
        moments, low, preferred_element_type=jnp.float32
    )


def packed_accel(total, packed, offset):
    row = row_index()
    even = row % 2 == 0
    folded = total[:8] + total[8:]
    halves = []
    for half in range(2):
        part = folded[:, half * LANES : (half + 1) * LANES]
        halves.append(jnp.where(even, part + pltpu.roll(part, 7, 0), part + pltpu.roll(part, 1, 0)))
    sums = jnp.where(even, halves[0], halves[1])
    mass_sum = over_components(jnp.where(row >= 6, sums, 0.0))
    return jnp.where(row >= 6, 0.0, sums - (packed + offset) * mass_sum)


def step_kernel(
    sizes,
    positions,
    velocities,
    mass,
    counts,
    moved_out,
    place_in,
    speed_in,
    mass_in,
    count_in,
    bins,
    targets,
    total,
    input_sem,
    send_sem,
    recv_sem,
):
    inputs = [
        pltpu.make_async_copy(source, target, input_sem.at[i])
        for i, (source, target) in enumerate(
            ((positions, place_in), (mass, mass_in), (counts, count_in), (velocities, speed_in))
        )
    ]
    for load in inputs:
        load.start()

    me = [lax.axis_index(name) for name in ("gx", "gy", "gz")]
    near = 1 - 2 * (me[0] % 2)
    near_y = 1 - 2 * (me[1] % 2)
    shift_z = (0, 1, -1)

    def neighbour(xi, yi, zi):
        dx = near * (xi % 2) - near * (xi // 2)
        dy = near_y * (yi % 2) - near_y * (yi // 2)
        return tuple(lax.rem(at + d + size, size) for at, d, size in zip(me, (dx, dy, shift_z[zi]), sizes))

    order = ((0, 0), (1, 0), (0, 1), (1, 1), (0, 2), (1, 2), (2, 1), (2, 2), (2, 0))
    peers = [(xi, yi, zi) for xi, yi in reversed(order) for zi in range(3) if (xi, yi, zi) != (0, 0, 0)]

    barrier = pltpu.get_barrier_semaphore()
    for peer in peers:
        pl.semaphore_signal(barrier, inc=1, device_id=neighbour(*peer), device_id_type=MESH)

    row = row_index()
    lane = lax.broadcasted_iota(jnp.int32, (8, LANES), 1)
    slot = lane + LANES * (row % 2)
    own_offset = [frame_offset(row, -0.5, -0.5, b - 1.0) for b in range(2)]
    for load in inputs:
        load.wait()
    speed = []
    for b in range(2):
        place_rows = [place_in[c, 0, 0, b : b + 1, h * LANES : (h + 1) * LANES] for c in range(3) for h in range(2)]
        mass_rows = [mass_in[0, 0, b : b + 1, h * LANES : (h + 1) * LANES] for h in range(2)]
        packed = jnp.concatenate(place_rows + mass_rows, axis=0)
        bins[0, 0, 1 + b] = jnp.where((row < 6) | (slot < count_in[0, 0, b]), packed, 0.0)
        speed_rows = [speed_in[c, 0, 0, b : b + 1, h * LANES : (h + 1) * LANES] for c in range(3) for h in range(2)]
        speed.append(jnp.concatenate(speed_rows + [jnp.zeros((2, LANES), jnp.float32)], axis=0))

    copies = []
    for sub in range(SUBCYCLES):

        def send():
            for xi, yi, zi in peers:
                column = order.index((xi, yi))
                rows = pl.ds(0, 8 if sub == 0 else 6)
                source = bins.at[sub, 0, pl.ds((1, 2, 1)[zi], 2 if zi == 0 else 1), rows]
                target = bins.at[sub, column, pl.ds((1, 0, 3)[zi], 2 if zi == 0 else 1), rows]
                copy = pltpu.make_async_remote_copy(
                    src_ref=source,
                    dst_ref=target,
                    send_sem=send_sem.at[sub, column, zi],
                    recv_sem=recv_sem.at[sub, column, zi],
                    device_id=neighbour(xi, yi, zi),
                    device_id_type=MESH,
                )
                copy.start()
                copies.append(copy)

        def arrived(column, zi):
            place = bins.at[sub, column, pl.ds((1, 0, 3)[zi], 2 if zi == 0 else 1), pl.ds(0, 8 if sub == 0 else 6)]
            pltpu.make_async_remote_copy(
                src_ref=place,
                dst_ref=place,
                send_sem=send_sem.at[sub, column, zi],
                recv_sem=recv_sem.at[sub, column, zi],
                device_id=neighbour(0, 0, 1),
                device_id_type=MESH,
            ).wait_recv()

        def column_sums(column, slots, sums):
            xi, yi = order[column]
            offset_x = (near * (xi % 2) - near * (xi // 2)).astype(jnp.float32) - 0.5 if xi else -0.5
            offset_y = (near_y * (yi % 2) - near_y * (yi // 2)).astype(jnp.float32) - 0.5 if yi else -0.5
            sums = list(sums)
            for z in slots:
                packed = bins[sub, column, z]
                if sub > 0:
                    packed = jnp.where(row < 6, packed, bins[0, column, z])
                features, moments = source_features(packed, frame_offset(row, offset_x, offset_y, z - 2.0))
                for b in range(2):
                    if abs(z - 1 - b) <= 1:
                        value = pair_sums(features, moments, targets[b])
                        sums[b] = value if sums[b] is None else sums[b] + value
            return sums

        def accumulate(group):
            for column, inner in group:
                for zi in (0,) if inner else (1, 2):
                    if (column, zi) != (0, 0):
                        arrived(column, zi)
            sums = [None, None]
            for column, inner in group:
                sums = column_sums(column, (1, 2) if inner else (0, 3), sums)
            for b in range(2):
                total[b] += sums[b]

        if sub == 0:
            for b in range(2):
                targets[b] = target_features(bins[sub, 0, 1 + b], own_offset[b])
            total[...] = jnp.zeros_like(total)
            accumulate(GROUPS[0])
            pl.semaphore_wait(barrier, len(peers))
            send()
        else:
            send()
            for b in range(2):
                targets[b] = target_features(bins[sub, 0, 1 + b], own_offset[b])
            total[...] = jnp.zeros_like(total)
            accumulate(GROUPS[0])

        for group in GROUPS[1:]:
            accumulate(group)

        for b in range(2):
            packed = bins[sub, 0, 1 + b]
            accel = packed_accel(total[b], packed, own_offset[b])
            speed[b] = speed[b] + time_step * accel
            moved = jnp.clip(packed + time_step * speed[b], 0.0, 1.0)
            if sub + 1 < SUBCYCLES:
                bins[sub + 1, 0, 1 + b] = jnp.where(row < 6, moved, packed)
            else:
                occupied = slot < count_in[0, 0, b]
                moved = jnp.where(occupied, moved, 0.0)
                final_speed = jnp.where(occupied, speed[b], 0.0)
                for c in range(3):
                    for h in range(2):
                        r = 2 * c + h
                        moved_out[c, 0, 0, b : b + 1, h * LANES : (h + 1) * LANES] = moved[r : r + 1]
                        moved_out[3 + c, 0, 0, b : b + 1, h * LANES : (h + 1) * LANES] = final_speed[r : r + 1]

    for copy in copies:
        copy.wait_send()


def solution(mesh):
    placed = (
        P(None, "gx", "gy", "gz", None),
        P(None, "gx", "gy", "gz", None),
        P("gx", "gy", "gz", None),
        P("gx", "gy", "gz"),
    )
    sizes = tuple(mesh.shape[name] for name in ("gx", "gy", "gz"))

    def on_device(positions, velocities, mass, counts):
        anywhere = pl.BlockSpec(memory_space=pl.ANY)
        moved = pl.pallas_call(
            functools.partial(step_kernel, sizes),
            out_shape=pltpu.VMEM((6,) + positions.shape[1:], jnp.float32),
            in_specs=[anywhere] * 4,
            out_specs=pl.BlockSpec(memory_space=pltpu.VMEM),
            scratch_shapes=[
                pltpu.VMEM(positions.shape, jnp.float32),
                pltpu.VMEM(velocities.shape, jnp.float32),
                pltpu.VMEM(mass.shape, jnp.float32),
                pltpu.SMEM(counts.shape, jnp.int32),
                pltpu.VMEM((SUBCYCLES, 9, 4, 8, LANES), jnp.float32),
                pltpu.VMEM((2, 32, 4 * LANES), jnp.bfloat16),
                pltpu.VMEM((2, 16, 2 * LANES), jnp.float32),
                pltpu.SemaphoreType.DMA((4,)),
                pltpu.SemaphoreType.DMA((SUBCYCLES, 9, 3)),
                pltpu.SemaphoreType.DMA((SUBCYCLES, 9, 3)),
            ],
            compiler_params=pltpu.CompilerParams(collective_id=0, has_side_effects=True),
        )(positions, velocities, mass, counts)
        return moved[:3], moved[3:]

    return jax.shard_map(
        on_device,
        mesh=mesh,
        in_specs=placed,
        out_specs=(P(None, "gx", "gy", "gz", None), P(None, "gx", "gy", "gz", None)),
        check_vma=False,
    )
```
